32 devices in a mesh: expert: 4 (over y, x), shard: 8 (over z, core).
Axes of the slice: x: 2, y: 2, z: 4, core: 2. Of those that a mesh axis runs over, the one named last changes fastest.
Arguments:
- tokens: bfloat16 [256, 4096], P(('expert', 'shard')), may hold values from -6 to 6
- cotangent: bfloat16 [256, 4096], P(('expert', 'shard')), may hold values from -6 to 6
- expert_ids: int32 [256, 2], P(('expert', 'shard')), may hold values from 0 to 3, as said below
- slot_ids: int32 [256, 2], P(('expert', 'shard')), may hold values from 0 to 3, as said below
- route_weight: float32 [256, 2], P(('expert', 'shard')), may hold values from 0.1 to 1
- w_gate: bfloat16 [4, 4096, 7168], P('expert', 'shard'), may hold values from -0.09375 to 0.09375
- w_up: bfloat16 [4, 4096, 7168], P('expert', 'shard'), may hold values from -0.09375 to 0.09375
- w_down: bfloat16 [4, 4096, 7168], P('expert', 'shard'), may hold values from -0.0625 to 0.0625
Outputs:
- layer_out: bfloat16 [256, 4096], P(('expert', 'shard'))
- d_tokens: bfloat16 [256, 4096], P(('expert', 'shard'))
- grad_gate: bfloat16 [4, 4096, 7168], P('expert', 'shard')
- grad_up: bfloat16 [4, 4096, 7168], P('expert', 'shard')
- grad_down: bfloat16 [4, 4096, 7168], P('expert', 'shard')
The draws below stay inside these ranges and needn't reach their ends.
Inputs may be any that keep to these rules, and one draw needn't show every extreme that they name: `expert_ids`: A token's two ids differ. Among the 8 tokens of one block no expert is named more than 4 times, and in every draw, for each index along shard, one expert is named exactly 4 times in each of the 4 blocks that share that index. Assignment k of a token takes slot slot_ids[., k] of the expert expert_ids[., k]; the assignments of one block to one expert have distinct slots.
All inputs are finite; a program needn't handle non-finite values.
Results may differ from the reference program's by a relative error of at most 0.019.
Values may be sent and summed in bfloat16 or wider, within the bound.
A program may use at most 128 MiB of HBM per device.

```python
import jax
import jax.numpy as jnp
from jax import lax

D = 4096
FFW = 7168
TOK_DEV = 8
EXPERTS = 4
SHARDS = 8
BLOCKS = 32
TOKENS = 256
CAP = 4
ROWS = 128


def route_tables(key):
    base_key = jax.random.fold_in(key, 1234)
    key_hot, key_bias, key_noise, key_order, key_swap = jax.random.split(base_key, 5)
    cell_count = EXPERTS * CAP
    hot_shard = jax.random.randint(key_hot, (SHARDS,), 0, EXPERTS)
    hot_block = jnp.tile(hot_shard, BLOCKS // SHARDS)
    expert_bias = jax.random.randint(key_bias, (BLOCKS, EXPERTS), 0, 4)
    noise = jax.random.randint(key_noise, (BLOCKS, cell_count), 0, 65536)
    cell_ids = jnp.arange(cell_count, dtype=jnp.int32)
    cell_expert = cell_ids // CAP
    boost = (cell_expert[None, :] == hot_block[:, None]).astype(jnp.int32) * 2 ** 28
    scores = (noise + expert_bias[:, cell_expert] * 65536) * cell_count + cell_ids[None, :] + boost
    chosen = lax.top_k(scores, 2 * TOK_DEV)[1]
    chosen = jnp.sort(chosen, axis=1)
    paired = jnp.stack([chosen[:, :TOK_DEV], chosen[:, TOK_DEV:]], axis=-1)
    order_keys = jax.random.randint(key_order, (BLOCKS, TOK_DEV), 0, 65536) * TOK_DEV + jnp.arange(TOK_DEV, dtype=jnp.int32)[None, :]
    order = jnp.argsort(order_keys, axis=1)
    paired = jnp.take_along_axis(paired, order[:, :, None], axis=1)
    swapped = jax.random.randint(key_swap, (BLOCKS, TOK_DEV, 1), 0, 2)
    paired = jnp.where(swapped == 1, paired[:, :, ::-1], paired)
    paired = paired.reshape(BLOCKS * TOK_DEV, 2).astype(jnp.int32)
    return (paired // CAP, paired % CAP)


def draw_expert_ids(key, part):
    return route_tables(key)[0]


def draw_slot_ids(key, part):
    return route_tables(key)[1]


def block_levels(key, dims, cuts, low, high):
    def one(dim, shards_of):
        heights = jax.random.uniform(jax.random.fold_in(jax.random.fold_in(key, 6), dim), (shards_of,), jnp.float32, low / len(cuts), high / len(cuts))
        return jnp.repeat(jnp.exp(heights), dims[dim] // shards_of).reshape((-1,) + (1,) * (len(dims) - dim - 1))

    level = one(*cuts[0])
    for cut in cuts[1:]:
        level = level * one(*cut)
    return level


def centred(rng, dims, scale, bound, shards=(), kind=jnp.bfloat16):
    drawn = scale * jax.random.normal(rng, dims, jnp.float32)
    if shards:
        drawn = drawn * block_levels(rng, dims, shards, -0.22, 0.18)
    return jnp.clip(drawn, -bound, bound).astype(kind)


def setup_inputs(seed: int = 0) -> dict:
    streams_of = jax.random.split(jax.random.key(seed), 9)
    return {
        "tokens": centred(streams_of[0], (TOKENS, D), 1.0, 6.0, ((0, 32),)),
        "cotangent": centred(streams_of[1], (TOKENS, D), 1.0, 6.0, ((0, 32),)),
        "expert_ids": draw_expert_ids(jax.random.fold_in(streams_of[8], 71), 0),
        "slot_ids": draw_slot_ids(jax.random.fold_in(streams_of[8], 71), 0),
        "route_weight": jnp.clip(0.1 + 0.9 * jax.random.uniform(streams_of[4], (TOKENS, 2), jnp.float32) ** block_levels(streams_of[4], (TOKENS, 2), ((0, 32),), -0.2, 0.2), 0.1, 1.0),
        "w_gate": centred(streams_of[5], (EXPERTS, D, FFW), D ** -0.5, 0.09375, ((0, 4), (1, 8))),
        "w_up": centred(streams_of[6], (EXPERTS, D, FFW), D ** -0.5, 0.09375, ((0, 4), (1, 8))),
        "w_down": centred(streams_of[7], (EXPERTS, D, FFW), FFW ** -0.5, 0.0625, ((0, 4), (1, 8))),
    }


def silu_parts(gate_value):
    logistic = jax.nn.sigmoid(gate_value)
    return gate_value * logistic, logistic * (1.0 + gate_value * (1.0 - logistic))


def grouped_sum(pairs):
    row_count = pairs[0][0].shape[0]
    width = FFW // SHARDS
    partials = jnp.zeros((SHARDS, row_count, D), jnp.float32)
    for left_side, right_side in pairs:
        left_group = left_side.astype(jnp.float32).reshape(row_count, SHARDS, width)
        right_group = right_side.astype(jnp.float32).reshape(D, SHARDS, width)
        partials = partials + jnp.einsum("rsf,dsf->srd", left_group, right_group, precision=lax.Precision.HIGHEST)
    rounded = lax.optimization_barrier(partials.astype(jnp.bfloat16)).astype(jnp.float32)
    return jnp.sum(rounded, axis=0)


def expert_pass(group_rows, d_rows, gate_matrix, up_matrix, down_matrix):
    gate_value = jnp.dot(group_rows, gate_matrix, preferred_element_type=jnp.float32)
    up_value = jnp.dot(group_rows, up_matrix, preferred_element_type=jnp.float32)
    activation, silu_slope = silu_parts(gate_value)
    hidden = (activation * up_value).astype(jnp.bfloat16)
    expert_out = grouped_sum([(hidden, down_matrix)]).astype(jnp.bfloat16)
    d_hidden = jnp.dot(d_rows, down_matrix, preferred_element_type=jnp.float32)
    grad_down = jnp.dot(d_rows.T, hidden, preferred_element_type=jnp.float32).astype(jnp.bfloat16)
    d_gate = (d_hidden * up_value * silu_slope).astype(jnp.bfloat16)
    d_up = (d_hidden * activation).astype(jnp.bfloat16)
    grad_gate = jnp.dot(group_rows.T, d_gate, preferred_element_type=jnp.float32).astype(jnp.bfloat16)
    grad_up = jnp.dot(group_rows.T, d_up, preferred_element_type=jnp.float32).astype(jnp.bfloat16)
    d_expert = grouped_sum([(d_gate, gate_matrix), (d_up, up_matrix)]).astype(jnp.bfloat16)
    return expert_out, d_expert, grad_gate, grad_up, grad_down


def by_expert(slot_rows):
    shaped = slot_rows.reshape(BLOCKS, EXPERTS, CAP, D)
    return jnp.transpose(shaped, (1, 0, 2, 3)).reshape(EXPERTS, ROWS, D)


def by_block(expert_rows):
    shaped = expert_rows.reshape(EXPERTS, BLOCKS, CAP, D)
    return jnp.transpose(shaped, (1, 0, 2, 3)).reshape(BLOCKS, EXPERTS * CAP, D).astype(jnp.float32)


def reference(tokens, cotangent, expert_ids, slot_ids, route_weight, w_gate, w_up, w_down):
    slot_index = expert_ids * CAP + slot_ids
    columns = jnp.arange(EXPERTS * CAP, dtype=jnp.int32)
    slot_match = (slot_index[:, :, None] == columns[None, None, :]).astype(jnp.float32)
    dispatch = jnp.sum(slot_match, axis=1).reshape(BLOCKS, TOK_DEV, EXPERTS * CAP)
    combine = jnp.sum(slot_match * route_weight[:, :, None], axis=1).reshape(BLOCKS, TOK_DEV, EXPERTS * CAP)
    token_blocks = tokens.astype(jnp.float32).reshape(BLOCKS, TOK_DEV, D)
    cotangent_blocks = cotangent.astype(jnp.float32).reshape(BLOCKS, TOK_DEV, D)
    x_slots = jnp.einsum("btc,btd->bcd", dispatch, token_blocks, precision=lax.Precision.HIGHEST).astype(jnp.bfloat16)
    d_slots = jnp.einsum("btc,btd->bcd", combine, cotangent_blocks, precision=lax.Precision.HIGHEST).astype(jnp.bfloat16)
    results = lax.map(lambda inputs: expert_pass(*inputs), (by_expert(x_slots), by_expert(d_slots), w_gate, w_up, w_down))
    expert_out, d_expert, grad_gate, grad_up, grad_down = results
    layer_out = jnp.einsum("btc,bcd->btd", combine, by_block(expert_out), precision=lax.Precision.HIGHEST)
    d_tokens = jnp.einsum("btc,bcd->btd", dispatch, by_block(d_expert), precision=lax.Precision.HIGHEST)
    layer_out = layer_out.reshape(TOKENS, D).astype(jnp.bfloat16)
    d_tokens = d_tokens.reshape(TOKENS, D).astype(jnp.bfloat16)
    return layer_out, d_tokens, grad_gate, grad_up, grad_down
```

```python
import jax
import jax.numpy as jnp
from jax import lax
from jax.sharding import PartitionSpec as P

CAP = 4
BOTH = ("expert", "shard")


def per_device(tokens, cotangent, expert_ids, slot_ids, route_weight, w_gate, w_up, w_down):
    experts = lax.axis_size("expert")
    shards = lax.axis_size("shard")
    slots_all = experts * CAP
    rows = experts * shards * CAP
    width = tokens.shape[1]
    part = width // shards
    slot_index = expert_ids * CAP + slot_ids
    columns = jnp.arange(slots_all, dtype=jnp.int32)
    slot_match = (slot_index[:, :, None] == columns[None, None, :]).astype(jnp.float32)
    dispatch = jnp.sum(slot_match, axis=1).astype(jnp.bfloat16)
    combine = jnp.sum(slot_match * route_weight[:, :, None], axis=1)
    x_slots = jnp.einsum("tc,td->cd", dispatch, tokens, preferred_element_type=jnp.float32).astype(
        jnp.bfloat16
    )
    d_slots = jnp.dot(
        combine.T, cotangent.astype(jnp.float32), precision=lax.Precision.HIGHEST
    ).astype(jnp.bfloat16)

    def send(slots):
        pieces = slots.reshape(experts, CAP, shards, part).transpose(0, 2, 1, 3)
        return pieces.reshape(experts * shards, CAP, part)

    arrived = lax.all_to_all(
        jnp.concatenate([send(x_slots), send(d_slots)], axis=1),
        BOTH, split_axis=0, concat_axis=0, tiled=True,
    )
    x_rows = arrived[:, :CAP].reshape(rows, part)
    d_rows = arrived[:, CAP:].reshape(rows, part)
    hidden_units = w_gate.shape[2]

    def partial(left, right):
        return jnp.dot(left, right, preferred_element_type=jnp.float32).astype(jnp.bfloat16)

    parts = jnp.concatenate(
        [partial(x_rows, w_gate[0]), partial(x_rows, w_up[0]), partial(d_rows, w_down[0])], axis=0
    )
    summed = lax.psum_scatter(parts, "shard", scatter_dimension=0, tiled=True)
    full = lax.all_gather(summed, "shard", axis=0, tiled=True).astype(jnp.float32)
    gate_value, up_value, d_hidden = full[:rows], full[rows : 2 * rows], full[2 * rows :]
    logistic = jax.nn.sigmoid(gate_value)
    activation = gate_value * logistic
    silu_slope = logistic * (1.0 + gate_value * (1.0 - logistic))
    hidden = (activation * up_value).astype(jnp.bfloat16)
    d_gate = (d_hidden * up_value * silu_slope).astype(jnp.bfloat16)
    d_up = (d_hidden * activation).astype(jnp.bfloat16)

    def back(left, right):
        return jnp.einsum("rf,df->rd", left, right, preferred_element_type=jnp.float32)

    expert_out = back(hidden, w_down[0]).astype(jnp.bfloat16)
    d_expert = (back(d_gate, w_gate[0]) + back(d_up, w_up[0])).astype(jnp.bfloat16)
    returned = lax.all_to_all(
        jnp.concatenate(
            [expert_out.reshape(-1, CAP, part), d_expert.reshape(-1, CAP, part)], axis=1
        ),
        BOTH, split_axis=0, concat_axis=0, tiled=True,
    )

    def take(pieces):
        return pieces.reshape(experts, shards, CAP, part).transpose(0, 2, 1, 3).reshape(slots_all, width)

    layer_out = jnp.dot(
        combine, take(returned[:, :CAP]).astype(jnp.float32), precision=lax.Precision.HIGHEST
    ).astype(jnp.bfloat16)
    d_tokens = jnp.dot(
        dispatch, take(returned[:, CAP:]), preferred_element_type=jnp.float32
    ).astype(jnp.bfloat16)

    def grad(left, right):
        return jnp.einsum("rd,rf->df", left, right, preferred_element_type=jnp.float32).astype(
            jnp.bfloat16
        )

    return (
        layer_out,
        d_tokens,
        grad(x_rows, d_gate)[None],
        grad(x_rows, d_up)[None],
        grad(d_rows, hidden)[None],
    )


def solution(mesh):
    tok = P(BOTH, None)
    wt = P("expert", "shard", None)
    return jax.shard_map(
        per_device,
        mesh=mesh,
        in_specs=(tok,) * 5 + (wt,) * 3,
        out_specs=(tok,) * 2 + (wt,) * 3,
        check_vma=False,
    )
```

```python
import functools

import jax
import jax.numpy as jnp
from jax import lax
from jax.experimental import pallas as pl
from jax.experimental.pallas import tpu as pltpu
from jax.sharding import PartitionSpec as P

CAP = 4
BOTH = ("expert", "shard")

MESH = pl.DeviceIdType.MESH
F32 = jnp.float32
BF16 = jnp.bfloat16
VMEM_BYTES = 60 * 2**20
SKEW = 2


def back(left, right):
    return lax.dot_general(left, right, (((1,), (1,)), ((), ())), preferred_element_type=F32)


def nonlinear(gate_value, up_value, d_hidden):
    logistic = jax.nn.sigmoid(gate_value)
    activation = gate_value * logistic
    silu_slope = logistic * (1.0 + gate_value * (1.0 - logistic))
    return (
        (activation * up_value).astype(BF16),
        (d_hidden * up_value * silu_slope).astype(BF16),
        (d_hidden * activation).astype(BF16),
    )


def core_kernel(
    chips, steps, width,
    x_ref, d_ref, gate_hbm, up_hbm, down_hbm,
    hidden_hbm, dgate_hbm, dup_hbm, out_ref, dexp_ref,
    weights, pair_tx, pair_rx, local, p_tx, p_rx, s_tx, s_rx, act, out_acc, dexp_acc,
    load_sem, pair_recv, p_recv, s_recv, act_recv, send_sem, store_sem,
):
    expert = lax.axis_index("expert")
    shard = lax.axis_index("shard")
    chip = shard // 2
    core = shard % 2
    mate = chip * 2 + 1 - core
    last = chips - 1
    right = lax.rem(shard + 2, 2 * chips)
    left = lax.rem(shard + 2 * last, 2 * chips)
    has_left = chip > 0
    has_right = chip < last
    lag_p = SKEW * chip
    lag_s = SKEW * (last - chip)
    lag = jnp.maximum(lag_p, lag_s)
    sources = (gate_hbm, up_hbm, down_hbm)
    targets = (hidden_hbm, dgate_hbm, dup_hbm)

    def columns(q):
        return pl.ds(pl.multiple_of(q * width, width), width)

    def load(j, carry):
        for side in (1 - core, core):
            q = side * steps + j
            for k in range(3):
                pltpu.make_async_copy(
                    sources[k].at[:, columns(q)], weights.at[q, k], load_sem.at[q]
                ).start()
        return carry

    lax.fori_loop(0, steps, load, 0)

    barrier = pltpu.get_barrier_semaphore()
    pl.semaphore_signal(barrier, inc=1, device_id=(expert, mate), device_id_type=MESH)

    @pl.when(has_left)
    def _():
        pl.semaphore_signal(barrier, inc=1, device_id=(expert, left), device_id_type=MESH)

    @pl.when(has_right)
    def _():
        pl.semaphore_signal(barrier, inc=1, device_id=(expert, right), device_id_type=MESH)

    @pl.when(jnp.logical_not(has_left))
    def _():
        p_rx[...] = jnp.zeros_like(p_rx)

    @pl.when(jnp.logical_not(has_right))
    def _():
        s_rx[...] = jnp.zeros_like(s_rx)

    out_acc[...] = jnp.zeros_like(out_acc)
    dexp_acc[...] = jnp.zeros_like(dexp_acc)
    pl.semaphore_wait(barrier, 1 + has_left.astype(jnp.int32) + has_right.astype(jnp.int32))

    def remote(src, dst, send, recv, target):
        return pltpu.make_async_remote_copy(
            src_ref=src, dst_ref=dst, send_sem=send, recv_sem=recv,
            device_id=(expert, target), device_id_type=MESH,
        )

    def pair_copy(j):
        return remote(pair_tx.at[j], pair_rx.at[j], send_sem.at[0], pair_recv.at[j], mate)

    def p_copy(j, k):
        return remote(p_tx.at[j, k], p_rx.at[j, k], send_sem.at[1], p_recv.at[j * 3 + k], right)

    def s_copy(j, k):
        return remote(s_tx.at[j, k], s_rx.at[j, k], send_sem.at[2], s_recv.at[j * 3 + k], left)

    def act_copy(j, side):
        q = side * steps + j
        return remote(act.at[q], act.at[q], send_sem.at[3], act_recv.at[j], mate)

    def partial(q, k):
        rows = d_ref if k == 2 else x_ref
        return jnp.dot(rows[...], weights[q, k], preferred_element_type=F32)

    def store(q):
        for k in range(3):
            pltpu.make_async_copy(act.at[q, k], targets[k].at[:, columns(q)], store_sem).start()

    def backward(q):
        out_acc[...] += back(act[q, 0], weights[q, 2])
        dexp_acc[...] += back(act[q, 1], weights[q, 0]) + back(act[q, 2], weights[q, 1])

    def within(j):
        return jnp.logical_and(j >= 0, j < steps)

    def tick(t, carry):
        @pl.when(t < steps)
        def _():
            for side in (1 - core, core):
                q = side * steps + t
                pltpu.make_async_copy(weights.at[q], weights.at[q], load_sem.at[q]).wait()
            q = (1 - core) * steps + t
            for k in range(3):
                pair_tx[t, k] = partial(q, k).astype(BF16)
            pair_copy(t).start()
            q = core * steps + t
            for k in range(3):
                local[t, k] = partial(q, k)

        j = t - 1

        @pl.when(within(j))
        def _():
            pair_copy(j).wait_recv()
            for k in range(3):
                local[j, k] += pair_rx[j, k].astype(F32)

        jp = t - 1 - lag_p

        @pl.when(within(jp))
        def _():
            for k in range(3):
                @pl.when(has_left)
                def _():
                    p_copy(jp, k).wait_recv()

                @pl.when(has_right)
                def _():
                    p_tx[jp, k] = (local[jp, k] + p_rx[jp, k].astype(F32)).astype(BF16)
                    p_copy(jp, k).start()

        js = t - 1 - lag_s

        @pl.when(within(js))
        def _():
            for k in range(3):
                @pl.when(has_right)
                def _():
                    s_copy(js, k).wait_recv()

                @pl.when(has_left)
                def _():
                    s_tx[js, k] = (local[js, k] + s_rx[js, k].astype(F32)).astype(BF16)
                    s_copy(js, k).start()

        jf = t - 1 - lag

        @pl.when(within(jf))
        def _():
            q = core * steps + jf
            total = [
                local[jf, k] + p_rx[jf, k].astype(F32) + s_rx[jf, k].astype(F32) for k in range(3)
            ]
            for k, value in enumerate(nonlinear(*total)):
                act[q, k] = value
            act_copy(jf, core).start()
            store(q)
            backward(q)

        jb = jf - 1

        @pl.when(within(jb))
        def _():
            q = (1 - core) * steps + jb
            act_copy(jb, 1 - core).wait_recv()
            store(q)
            backward(q)

        return carry

    lax.fori_loop(0, steps + SKEW * last + 2, tick, 0)
    out_ref[...] = out_acc[...].astype(BF16)
    dexp_ref[...] = dexp_acc[...].astype(BF16)
    remote(pair_tx, pair_rx, send_sem.at[0], pair_recv.at[0], mate).wait_send()

    @pl.when(has_right)
    def _():
        remote(p_tx, p_rx, send_sem.at[1], p_recv.at[0], right).wait_send()

    @pl.when(has_left)
    def _():
        remote(s_tx, s_rx, send_sem.at[2], s_recv.at[0], left).wait_send()

    half = act.at[pl.ds(0, steps)]
    remote(half, half, send_sem.at[3], act_recv.at[0], mate).wait_send()
    pltpu.make_async_copy(act, act, store_sem).wait()


def plan(shards, rows, part, units):
    if shards % 2 or units % 256:
        return None
    for width in (256, 128):
        if (units // 2) % width:
            continue
        held = 3 * part * units * 2 + 3 * rows * units * (2 + 2 + 6 * 1) + 2 * rows * part * (4 + 8)
        if held <= 55 * 2**20:
            return width
    return None


def expert_core(x_rows, d_rows, w_gate, w_up, w_down, width):
    shards = lax.axis_size("shard")
    rows, part = x_rows.shape
    units = w_gate.shape[1]
    steps = units // 2 // width
    chips = shards // 2
    anywhere = pl.BlockSpec(memory_space=pl.ANY)
    vmem = pl.BlockSpec(memory_space=pltpu.VMEM)
    block = (steps, 3, rows, width)
    dma = pltpu.SemaphoreType.DMA
    return pl.pallas_call(
        functools.partial(core_kernel, chips, steps, width),
        out_shape=[jax.ShapeDtypeStruct((rows, units), BF16)] * 3
        + [jax.ShapeDtypeStruct((rows, part), BF16)] * 2,
        in_specs=[vmem] * 2 + [anywhere] * 3,
        out_specs=[anywhere] * 3 + [vmem] * 2,
        scratch_shapes=[
            pltpu.VMEM((2 * steps, 3, part, width), BF16),
            pltpu.VMEM(block, BF16),
            pltpu.VMEM(block, BF16),
            pltpu.VMEM(block, F32),
            pltpu.VMEM(block, BF16),
            pltpu.VMEM(block, BF16),
            pltpu.VMEM(block, BF16),
            pltpu.VMEM(block, BF16),
            pltpu.VMEM((2 * steps, 3, rows, width), BF16),
            pltpu.VMEM((rows, part), F32),
            pltpu.VMEM((rows, part), F32),
            dma((2 * steps,)),
            dma((steps,)),
            dma((3 * steps,)),
            dma((3 * steps,)),
            dma((steps,)),
            dma((4,)),
            dma,
        ],
        compiler_params=pltpu.CompilerParams(
            collective_id=0, has_side_effects=True, vmem_limit_bytes=VMEM_BYTES
        ),
        name="expert_core",
    )(x_rows, d_rows, w_gate, w_up, w_down)


def expert_plain(x_rows, d_rows, w_gate, w_up, w_down):
    rows = x_rows.shape[0]

    def partial(left, right):
        return jnp.dot(left, right, preferred_element_type=F32).astype(BF16)

    parts = jnp.concatenate(
        [partial(x_rows, w_gate), partial(x_rows, w_up), partial(d_rows, w_down)], axis=0
    )
    summed = lax.psum_scatter(parts, "shard", scatter_dimension=0, tiled=True)
    full = lax.all_gather(summed, "shard", axis=0, tiled=True).astype(F32)
    hidden, d_gate, d_up = nonlinear(full[:rows], full[rows : 2 * rows], full[2 * rows :])
    expert_out = back(hidden, w_down).astype(BF16)
    d_expert = (back(d_gate, w_gate) + back(d_up, w_up)).astype(BF16)
    return hidden, d_gate, d_up, expert_out, d_expert


def per_device(tokens, cotangent, expert_ids, slot_ids, route_weight, w_gate, w_up, w_down):
    experts = lax.axis_size("expert")
    shards = lax.axis_size("shard")
    slots_all = experts * CAP
    rows = experts * shards * CAP
    width = tokens.shape[1]
    part = width // shards
    slot_index = expert_ids * CAP + slot_ids
    columns = jnp.arange(slots_all, dtype=jnp.int32)
    slot_match = (slot_index[:, :, None] == columns[None, None, :]).astype(jnp.float32)
    dispatch = jnp.sum(slot_match, axis=1).astype(jnp.bfloat16)
    combine = jnp.sum(slot_match * route_weight[:, :, None], axis=1)
    x_slots = jnp.einsum("tc,td->cd", dispatch, tokens, preferred_element_type=jnp.float32).astype(
        jnp.bfloat16
    )
    d_slots = jnp.dot(
        combine.T, cotangent.astype(jnp.float32), precision=lax.Precision.HIGHEST
    ).astype(jnp.bfloat16)

    def send(slots):
        pieces = slots.reshape(experts, CAP, shards, part).transpose(0, 2, 1, 3)
        return pieces.reshape(experts * shards, CAP, part)

    arrived = lax.all_to_all(
        jnp.concatenate([send(x_slots), send(d_slots)], axis=1),
        BOTH, split_axis=0, concat_axis=0, tiled=True,
    )
    x_rows = arrived[:, :CAP].reshape(rows, part)
    d_rows = arrived[:, CAP:].reshape(rows, part)
    hidden_units = w_gate.shape[2]

    width_step = plan(shards, rows, part, hidden_units)
    if width_step:
        hidden, d_gate, d_up, expert_out, d_expert = expert_core(
            x_rows, d_rows, w_gate[0], w_up[0], w_down[0], width_step
        )
    else:
        hidden, d_gate, d_up, expert_out, d_expert = expert_plain(
            x_rows, d_rows, w_gate[0], w_up[0], w_down[0]
        )
    returned = lax.all_to_all(
        jnp.concatenate(
            [expert_out.reshape(-1, CAP, part), d_expert.reshape(-1, CAP, part)], axis=1
        ),
        BOTH, split_axis=0, concat_axis=0, tiled=True,
    )

    def take(pieces):
        return pieces.reshape(experts, shards, CAP, part).transpose(0, 2, 1, 3).reshape(slots_all, width)

    layer_out = jnp.dot(
        combine, take(returned[:, :CAP]).astype(jnp.float32), precision=lax.Precision.HIGHEST
    ).astype(jnp.bfloat16)
    d_tokens = jnp.dot(
        dispatch, take(returned[:, CAP:]), preferred_element_type=jnp.float32
    ).astype(jnp.bfloat16)

    def grad(left, right):
        return jnp.einsum("rd,rf->df", left, right, preferred_element_type=jnp.float32).astype(
            jnp.bfloat16
        )

    return (
        layer_out,
        d_tokens,
        grad(x_rows, d_gate)[None],
        grad(x_rows, d_up)[None],
        grad(d_rows, hidden)[None],
    )


def solution(mesh):
    tok = P(BOTH, None)
    wt = P("expert", "shard", None)
    return jax.shard_map(
        per_device,
        mesh=mesh,
        in_specs=(tok,) * 5 + (wt,) * 3,
        out_specs=(tok,) * 2 + (wt,) * 3,
        check_vma=False,
    )
```

```python
import functools

import jax
import jax.numpy as jnp
from jax import lax
from jax.experimental import pallas as pl
from jax.experimental.pallas import tpu as pltpu
from jax.sharding import PartitionSpec as P

CAP = 4
BOTH = ("expert", "shard")

MESH = pl.DeviceIdType.MESH
F32 = jnp.float32
BF16 = jnp.bfloat16
VMEM_BYTES = 60 * 2**20
SKEW = 2


def back(left, right):
    return lax.dot_general(left, right, (((1,), (1,)), ((), ())), preferred_element_type=F32)


def nonlinear(gate_value, up_value, d_hidden):
    logistic = jax.nn.sigmoid(gate_value)
    activation = gate_value * logistic
    silu_slope = logistic * (1.0 + gate_value * (1.0 - logistic))
    return (
        (activation * up_value).astype(BF16),
        (d_hidden * up_value * silu_slope).astype(BF16),
        (d_hidden * activation).astype(BF16),
    )


def core_kernel(
    chips, steps, width,
    pieces_ref, gate_hbm, up_hbm, down_hbm,
    hidden_hbm, dgate_hbm, dup_hbm, x_ref, d_ref, results_ref,
    pieces_rx, weights, pair_tx, pair_rx, local, p_tx, p_rx, s_tx, s_rx, act, out_acc, dexp_acc,
    load_sem, piece_recv, pair_recv, p_recv, s_recv, act_recv, send_sem, store_sem,
):
    expert = lax.axis_index("expert")
    shard = lax.axis_index("shard")
    chip = shard // 2
    core = shard % 2
    mate = chip * 2 + 1 - core
    shards = 2 * chips
    me = expert * shards + shard
    devices = pieces_ref.shape[0]
    last = chips - 1
    right = lax.rem(shard + 2, 2 * chips)
    left = lax.rem(shard + 2 * last, 2 * chips)
    has_left = chip > 0
    has_right = chip < last
    lag_p = SKEW * chip
    lag_s = SKEW * (last - chip)
    lag = jnp.maximum(lag_p, lag_s)
    sources = (gate_hbm, up_hbm, down_hbm)
    targets = (hidden_hbm, dgate_hbm, dup_hbm)

    def columns(q):
        return pl.ds(pl.multiple_of(q * width, width), width)

    def load(j, carry):
        for side in (1 - core, core):
            q = side * steps + j
            for k in range(3):
                pltpu.make_async_copy(
                    sources[k].at[:, columns(q)], weights.at[q, k], load_sem.at[q]
                ).start()
        return carry

    lax.fori_loop(0, steps, load, 0)

    barrier = pltpu.get_barrier_semaphore()

    def greet(o, carry):
        other = lax.rem(me + o, devices)
        pl.semaphore_signal(
            barrier, inc=1, device_id=(other // shards, other % shards), device_id_type=MESH
        )
        return carry

    lax.fori_loop(1, devices, greet, 0)

    @pl.when(jnp.logical_not(has_left))
    def _():
        p_rx[...] = jnp.zeros_like(p_rx)

    @pl.when(jnp.logical_not(has_right))
    def _():
        s_rx[...] = jnp.zeros_like(s_rx)

    out_acc[...] = jnp.zeros_like(out_acc)
    dexp_acc[...] = jnp.zeros_like(dexp_acc)
    pieces_rx[me] = pieces_ref[me]
    pl.semaphore_wait(barrier, devices - 1)

    def remote(src, dst, send, recv, target):
        return pltpu.make_async_remote_copy(
            src_ref=src, dst_ref=dst, send_sem=send, recv_sem=recv,
            device_id=(expert, target), device_id_type=MESH,
        )

    def piece_copy(target, source):
        return pltpu.make_async_remote_copy(
            src_ref=pieces_ref.at[target], dst_ref=pieces_rx.at[source],
            send_sem=send_sem.at[4], recv_sem=piece_recv.at[source],
            device_id=(target // shards, target % shards), device_id_type=MESH,
        )

    def send_piece(o, carry):
        piece_copy(lax.rem(me + o, devices), me).start()
        return carry

    def await_piece(o, carry):
        other = lax.rem(me + o, devices)
        piece_copy(other, other).wait_recv()
        return carry

    lax.fori_loop(1, devices, send_piece, 0)
    lax.fori_loop(1, devices, await_piece, 0)
    tile_rows, half = pieces_ref.shape[1:]
    rows = devices * CAP
    mixed = pieces_rx[...].reshape(devices * tile_rows, half)
    halves = tile_rows // (2 * CAP)

    def picks(kind, h, transposed):
        shape = (devices * tile_rows, rows) if transposed else (rows, devices * tile_rows)
        slot = lax.broadcasted_iota(jnp.int32, shape, int(transposed))
        piece = lax.broadcasted_iota(jnp.int32, shape, 1 - int(transposed))
        wanted = slot // CAP * tile_rows + h * 2 * CAP + kind * CAP + slot % CAP
        return (piece == wanted).astype(F32).astype(BF16)

    for kind, ref in enumerate((x_ref, d_ref)):
        for h in range(halves):
            ref[:, h * half : (h + 1) * half] = jnp.dot(
                picks(kind, h, False), mixed, preferred_element_type=F32
            ).astype(BF16)

    def pair_copy(j):
        return remote(pair_tx.at[j], pair_rx.at[j], send_sem.at[0], pair_recv.at[j], mate)

    def p_copy(j, k):
        return remote(p_tx.at[j, k], p_rx.at[j, k], send_sem.at[1], p_recv.at[j * 3 + k], right)

    def s_copy(j, k):
        return remote(s_tx.at[j, k], s_rx.at[j, k], send_sem.at[2], s_recv.at[j * 3 + k], left)

    def act_copy(j, side):
        q = side * steps + j
        return remote(act.at[q], act.at[q], send_sem.at[3], act_recv.at[j], mate)

    def partial(q, k):
        rows = d_ref if k == 2 else x_ref
        return jnp.dot(rows[...], weights[q, k], preferred_element_type=F32)

    def store(q):
        for k in range(3):
            pltpu.make_async_copy(act.at[q, k], targets[k].at[:, columns(q)], store_sem).start()

    def backward(q):
        out_acc[...] += back(act[q, 0], weights[q, 2])
        dexp_acc[...] += back(act[q, 1], weights[q, 0]) + back(act[q, 2], weights[q, 1])

    def within(j):
        return jnp.logical_and(j >= 0, j < steps)

    def tick(t, carry):
        @pl.when(t < steps)
        def _():
            for side in (1 - core, core):
                q = side * steps + t
                pltpu.make_async_copy(weights.at[q], weights.at[q], load_sem.at[q]).wait()
            q = (1 - core) * steps + t
            for k in range(3):
                pair_tx[t, k] = partial(q, k).astype(BF16)
            pair_copy(t).start()
            q = core * steps + t
            for k in range(3):
                local[t, k] = partial(q, k)

        j = t - 1

        @pl.when(within(j))
        def _():
            pair_copy(j).wait_recv()
            for k in range(3):
                local[j, k] += pair_rx[j, k].astype(F32)

        jp = t - 1 - lag_p

        @pl.when(within(jp))
        def _():
            for k in range(3):
                @pl.when(has_left)
                def _():
                    p_copy(jp, k).wait_recv()

                @pl.when(has_right)
                def _():
                    p_tx[jp, k] = (local[jp, k] + p_rx[jp, k].astype(F32)).astype(BF16)
                    p_copy(jp, k).start()

        js = t - 1 - lag_s

        @pl.when(within(js))
        def _():
            for k in range(3):
                @pl.when(has_right)
                def _():
                    s_copy(js, k).wait_recv()

                @pl.when(has_left)
                def _():
                    s_tx[js, k] = (local[js, k] + s_rx[js, k].astype(F32)).astype(BF16)
                    s_copy(js, k).start()

        jf = t - 1 - lag

        @pl.when(within(jf))
        def _():
            q = core * steps + jf
            total = [
                local[jf, k] + p_rx[jf, k].astype(F32) + s_rx[jf, k].astype(F32) for k in range(3)
            ]
            for k, value in enumerate(nonlinear(*total)):
                act[q, k] = value
            act_copy(jf, core).start()
            store(q)
            backward(q)

        jb = jf - 1

        @pl.when(within(jb))
        def _():
            q = (1 - core) * steps + jb
            act_copy(jb, 1 - core).wait_recv()
            store(q)
            backward(q)

        return carry

    lax.fori_loop(0, steps + SKEW * last + 2, tick, 0)
    total = jnp.zeros((devices * tile_rows, half), F32)
    for kind, acc in enumerate((out_acc, dexp_acc)):
        for h in range(halves):
            total += jnp.dot(
                picks(kind, h, True),
                acc[:, h * half : (h + 1) * half].astype(BF16),
                preferred_element_type=F32,
            )
    results_ref[...] = total.astype(BF16).reshape(results_ref.shape)
    sent = pl.ds(0, devices - 1)
    pltpu.make_async_remote_copy(
        src_ref=pieces_ref.at[sent], dst_ref=pieces_rx.at[sent],
        send_sem=send_sem.at[4], recv_sem=piece_recv.at[0],
        device_id=(expert, mate), device_id_type=MESH,
    ).wait_send()
    remote(pair_tx, pair_rx, send_sem.at[0], pair_recv.at[0], mate).wait_send()

    @pl.when(has_right)
    def _():
        remote(p_tx, p_rx, send_sem.at[1], p_recv.at[0], right).wait_send()

    @pl.when(has_left)
    def _():
        remote(s_tx, s_rx, send_sem.at[2], s_recv.at[0], left).wait_send()

    mine = act.at[pl.ds(0, steps)]
    remote(mine, mine, send_sem.at[3], act_recv.at[0], mate).wait_send()
    pltpu.make_async_copy(act, act, store_sem).wait()


def plan(shards, rows, part, units):
    if shards % 2 or units % 256 or part % (16 // (2 * CAP) * 128):
        return None
    for width in (256, 128):
        if (units // 2) % width:
            continue
        held = 3 * part * units * 2 + 3 * rows * units * (2 + 2 + 6 * 1) + 2 * rows * part * (4 + 8)
        if held <= 55 * 2**20:
            return width
    return None


def expert_core(pieces, w_gate, w_up, w_down, width):
    shards = lax.axis_size("shard")
    devices = pieces.shape[0]
    rows = devices * CAP
    part, units = w_gate.shape
    steps = units // 2 // width
    chips = shards // 2
    anywhere = pl.BlockSpec(memory_space=pl.ANY)
    vmem = pl.BlockSpec(memory_space=pltpu.VMEM)
    block = (steps, 3, rows, width)
    dma = pltpu.SemaphoreType.DMA
    return pl.pallas_call(
        functools.partial(core_kernel, chips, steps, width),
        out_shape=[jax.ShapeDtypeStruct((rows, units), BF16)] * 3
        + [jax.ShapeDtypeStruct((rows, part), BF16)] * 2
        + [jax.ShapeDtypeStruct(pieces.shape, BF16)],
        in_specs=[vmem] + [anywhere] * 3,
        out_specs=[anywhere] * 3 + [vmem] * 3,
        scratch_shapes=[
            pltpu.VMEM(pieces.shape, BF16),
            pltpu.VMEM((2 * steps, 3, part, width), BF16),
            pltpu.VMEM(block, BF16),
            pltpu.VMEM(block, BF16),
            pltpu.VMEM(block, F32),
            pltpu.VMEM(block, BF16),
            pltpu.VMEM(block, BF16),
            pltpu.VMEM(block, BF16),
            pltpu.VMEM(block, BF16),
            pltpu.VMEM((2 * steps, 3, rows, width), BF16),
            pltpu.VMEM((rows, part), F32),
            pltpu.VMEM((rows, part), F32),
            dma((2 * steps,)),
            dma((devices,)),
            dma((steps,)),
            dma((3 * steps,)),
            dma((3 * steps,)),
            dma((steps,)),
            dma((5,)),
            dma,
        ],
        compiler_params=pltpu.CompilerParams(
            collective_id=0, has_side_effects=True, vmem_limit_bytes=VMEM_BYTES
        ),
        name="expert_core",
    )(pieces, w_gate, w_up, w_down)


def expert_plain(x_rows, d_rows, w_gate, w_up, w_down):
    rows = x_rows.shape[0]

    def partial(left, right):
        return jnp.dot(left, right, preferred_element_type=F32).astype(BF16)

    parts = jnp.concatenate(
        [partial(x_rows, w_gate), partial(x_rows, w_up), partial(d_rows, w_down)], axis=0
    )
    summed = lax.psum_scatter(parts, "shard", scatter_dimension=0, tiled=True)
    full = lax.all_gather(summed, "shard", axis=0, tiled=True).astype(F32)
    hidden, d_gate, d_up = nonlinear(full[:rows], full[rows : 2 * rows], full[2 * rows :])
    expert_out = back(hidden, w_down).astype(BF16)
    d_expert = (back(d_gate, w_gate) + back(d_up, w_up)).astype(BF16)
    return hidden, d_gate, d_up, expert_out, d_expert


def per_device(tokens, cotangent, expert_ids, slot_ids, route_weight, w_gate, w_up, w_down):
    experts = lax.axis_size("expert")
    shards = lax.axis_size("shard")
    slots_all = experts * CAP
    rows = experts * shards * CAP
    width = tokens.shape[1]
    part = width // shards
    slot_index = expert_ids * CAP + slot_ids
    columns = jnp.arange(slots_all, dtype=jnp.int32)
    slot_match = (slot_index[:, :, None] == columns[None, None, :]).astype(jnp.float32)
    dispatch = jnp.sum(slot_match, axis=1).astype(jnp.bfloat16)
    combine = jnp.sum(slot_match * route_weight[:, :, None], axis=1)
    x_slots = jnp.einsum("tc,td->cd", dispatch, tokens, preferred_element_type=jnp.float32).astype(
        jnp.bfloat16
    )
    d_slots = jnp.dot(
        combine.T, cotangent.astype(jnp.float32), precision=lax.Precision.HIGHEST
    ).astype(jnp.bfloat16)

    hidden_units = w_gate.shape[2]
    devices = experts * shards
    width_step = plan(shards, rows, part, hidden_units)
    halves = 16 // (2 * CAP) if width_step else 1

    both = jnp.stack([x_slots, d_slots]).reshape(
        2, experts, CAP, shards, halves, part // halves
    )
    pieces = both.transpose(1, 3, 4, 0, 2, 5).reshape(
        devices, halves * 2 * CAP, part // halves
    )
    if width_step:
        hidden, d_gate, d_up, x_rows, d_rows, results = expert_core(
            pieces, w_gate[0], w_up[0], w_down[0], width_step
        )
    else:
        arrived = lax.all_to_all(pieces, BOTH, split_axis=0, concat_axis=0, tiled=True)
        x_rows = arrived[:, :CAP].reshape(rows, part)
        d_rows = arrived[:, CAP:].reshape(rows, part)
        hidden, d_gate, d_up, expert_out, d_expert = expert_plain(
            x_rows, d_rows, w_gate[0], w_up[0], w_down[0]
        )
        results = jnp.concatenate(
            [expert_out.reshape(-1, CAP, part), d_expert.reshape(-1, CAP, part)], axis=1
        )
    returned = lax.all_to_all(results, BOTH, split_axis=0, concat_axis=0, tiled=True)
    returned = returned.reshape(experts, shards, halves, 2, CAP, part // halves)
    returned = returned.transpose(3, 0, 4, 1, 2, 5).reshape(2, slots_all, width)
    layer_out = jnp.dot(
        combine, returned[0].astype(jnp.float32), precision=lax.Precision.HIGHEST
    ).astype(jnp.bfloat16)
    d_tokens = jnp.dot(
        dispatch, returned[1], preferred_element_type=jnp.float32
    ).astype(jnp.bfloat16)

    def grad(left, right):
        return jnp.einsum("rd,rf->df", left, right, preferred_element_type=jnp.float32).astype(
            jnp.bfloat16
        )

    return (
        layer_out,
        d_tokens,
        grad(x_rows, d_gate)[None],
        grad(x_rows, d_up)[None],
        grad(d_rows, hidden)[None],
    )


def solution(mesh):
    tok = P(BOTH, None)
    wt = P("expert", "shard", None)
    return jax.shard_map(
        per_device,
        mesh=mesh,
        in_specs=(tok,) * 5 + (wt,) * 3,
        out_specs=(tok,) * 2 + (wt,) * 3,
        check_vma=False,
    )
```

```python
import functools

import jax
import jax.numpy as jnp
from jax import lax
from jax.experimental import pallas as pl
from jax.experimental.pallas import tpu as pltpu
from jax.sharding import PartitionSpec as P

CAP = 4
BOTH = ("expert", "shard")

MESH = pl.DeviceIdType.MESH
F32 = jnp.float32
BF16 = jnp.bfloat16
VMEM_BYTES = 60 * 2**20
SKEW = 2


def back(left, right):
    return lax.dot_general(left, right, (((1,), (1,)), ((), ())), preferred_element_type=F32)


def nonlinear(gate_value, up_value, d_hidden):
    logistic = jax.nn.sigmoid(gate_value)
    activation = gate_value * logistic
    silu_slope = logistic * (1.0 + gate_value * (1.0 - logistic))
    return (
        (activation * up_value).astype(BF16),
        (d_hidden * up_value * silu_slope).astype(BF16),
        (d_hidden * activation).astype(BF16),
    )


def core_kernel(
    chips, steps, width,
    tokens_ref, cotangent_ref, slot_ref, weight_ref, gate_hbm, up_hbm, down_hbm,
    hidden_hbm, dgate_hbm, dup_hbm, x_ref, d_ref, results_ref,
    pieces_ref, pieces_rx, weights, pair_tx, pair_rx, local, p_tx, p_rx, s_tx, s_rx, act, out_acc, dexp_acc,
    load_sem, piece_recv, pair_recv, p_recv, s_recv, act_recv, send_sem, store_sem,
):
    expert = lax.axis_index("expert")
    shard = lax.axis_index("shard")
    chip = shard // 2
    core = shard % 2
    mate = chip * 2 + 1 - core
    shards = 2 * chips
    me = expert * shards + shard
    devices = pieces_ref.shape[0]
    last = chips - 1
    right = lax.rem(shard + 2, 2 * chips)
    left = lax.rem(shard + 2 * last, 2 * chips)
    has_left = chip > 0
    has_right = chip < last
    lag_p = SKEW * chip
    lag_s = SKEW * (last - chip)
    lag = jnp.maximum(lag_p, lag_s)
    sources = (gate_hbm, up_hbm, down_hbm)
    targets = (hidden_hbm, dgate_hbm, dup_hbm)

    def columns(q):
        return pl.ds(pl.multiple_of(q * width, width), width)

    def load(j, carry):
        for side in (1 - core, core):
            q = side * steps + j
            for k in range(3):
                pltpu.make_async_copy(
                    sources[k].at[:, columns(q)], weights.at[q, k], load_sem.at[q]
                ).start()
        return carry

    lax.fori_loop(0, steps, load, 0)

    barrier = pltpu.get_barrier_semaphore()

    def greet(o, carry):
        other = lax.rem(me + o, devices)
        pl.semaphore_signal(
            barrier, inc=1, device_id=(other // shards, other % shards), device_id_type=MESH
        )
        return carry

    lax.fori_loop(1, devices, greet, 0)

    @pl.when(jnp.logical_not(has_left))
    def _():
        p_rx[...] = jnp.zeros_like(p_rx)

    @pl.when(jnp.logical_not(has_right))
    def _():
        s_rx[...] = jnp.zeros_like(s_rx)

    out_acc[...] = jnp.zeros_like(out_acc)
    dexp_acc[...] = jnp.zeros_like(dexp_acc)
    tile_rows, half = pieces_ref.shape[1:]
    block = 2 * CAP
    halves = tile_rows // block
    line = lax.broadcasted_iota(
        jnp.int32, (tokens_ref.shape[0], devices // shards * block), 1
    )
    wanted = line // block * CAP + line % CAP
    is_token = line % block < CAP
    by_token = jnp.zeros(line.shape, F32)
    by_cotangent = jnp.zeros(line.shape, F32)
    for k in range(slot_ref.shape[1]):
        match = (slot_ref[:, k : k + 1] == wanted).astype(F32)
        by_token += jnp.where(is_token, match, 0.0)
        by_cotangent += jnp.where(is_token, 0.0, match * weight_ref[:, k : k + 1])

    def slot_rows(factors, values):
        return lax.dot_general(
            factors, values.astype(F32), (((0,), (0,)), ((), ())),
            precision=lax.Precision.HIGHEST, preferred_element_type=F32,
        )

    for s in range(shards):
        for h in range(halves):
            begin = (s * halves + h) * half
            span = slice(begin, begin + half)
            mixed_rows = slot_rows(by_token, tokens_ref[:, span]) + slot_rows(
                by_cotangent, cotangent_ref[:, span]
            )
            for e in range(devices // shards):
                pieces_ref[e * shards + s, h * block : (h + 1) * block, :] = mixed_rows[
                    e * block : (e + 1) * block
                ].astype(BF16)
    pieces_rx[me] = pieces_ref[me]
    pl.semaphore_wait(barrier, devices - 1)

    def remote(src, dst, send, recv, target):
        return pltpu.make_async_remote_copy(
            src_ref=src, dst_ref=dst, send_sem=send, recv_sem=recv,
            device_id=(expert, target), device_id_type=MESH,
        )

    def piece_copy(target, source):
        return pltpu.make_async_remote_copy(
            src_ref=pieces_ref.at[target], dst_ref=pieces_rx.at[source],
            send_sem=send_sem.at[4], recv_sem=piece_recv.at[source],
            device_id=(target // shards, target % shards), device_id_type=MESH,
        )

    def send_piece(o, carry):
        piece_copy(lax.rem(me + o, devices), me).start()
        return carry

    def await_piece(o, carry):
        other = lax.rem(me + o, devices)
        piece_copy(other, other).wait_recv()
        return carry

    lax.fori_loop(1, devices, send_piece, 0)
    lax.fori_loop(1, devices, await_piece, 0)
    rows = devices * CAP
    mixed = pieces_rx[...].reshape(devices * tile_rows, half)

    def picks(kind, h, transposed):
        shape = (devices * tile_rows, rows) if transposed else (rows, devices * tile_rows)
        slot = lax.broadcasted_iota(jnp.int32, shape, int(transposed))
        piece = lax.broadcasted_iota(jnp.int32, shape, 1 - int(transposed))
        wanted = slot // CAP * tile_rows + h * 2 * CAP + kind * CAP + slot % CAP
        return (piece == wanted).astype(F32).astype(BF16)

    for kind, ref in enumerate((x_ref, d_ref)):
        for h in range(halves):
            ref[:, h * half : (h + 1) * half] = jnp.dot(
                picks(kind, h, False), mixed, preferred_element_type=F32
            ).astype(BF16)

    def pair_copy(j):
        return remote(pair_tx.at[j], pair_rx.at[j], send_sem.at[0], pair_recv.at[j], mate)

    def p_copy(j, k):
        return remote(p_tx.at[j, k], p_rx.at[j, k], send_sem.at[1], p_recv.at[j * 3 + k], right)

    def s_copy(j, k):
        return remote(s_tx.at[j, k], s_rx.at[j, k], send_sem.at[2], s_recv.at[j * 3 + k], left)

    def act_copy(j, side):
        q = side * steps + j
        return remote(act.at[q], act.at[q], send_sem.at[3], act_recv.at[j], mate)

    def partial(q, k):
        rows = d_ref if k == 2 else x_ref
        return jnp.dot(rows[...], weights[q, k], preferred_element_type=F32)

    def store(q):
        for k in range(3):
            pltpu.make_async_copy(act.at[q, k], targets[k].at[:, columns(q)], store_sem).start()

    def backward(q):
        out_acc[...] += back(act[q, 0], weights[q, 2])
        dexp_acc[...] += back(act[q, 1], weights[q, 0]) + back(act[q, 2], weights[q, 1])

    def within(j):
        return jnp.logical_and(j >= 0, j < steps)

    def tick(t, carry):
        @pl.when(t < steps)
        def _():
            for side in (1 - core, core):
                q = side * steps + t
                pltpu.make_async_copy(weights.at[q], weights.at[q], load_sem.at[q]).wait()
            q = (1 - core) * steps + t
            for k in range(3):
                pair_tx[t, k] = partial(q, k).astype(BF16)
            pair_copy(t).start()
            q = core * steps + t
            for k in range(3):
                local[t, k] = partial(q, k)

        j = t - 1

        @pl.when(within(j))
        def _():
            pair_copy(j).wait_recv()
            for k in range(3):
                local[j, k] += pair_rx[j, k].astype(F32)

        jp = t - 1 - lag_p

        @pl.when(within(jp))
        def _():
            for k in range(3):
                @pl.when(has_left)
                def _():
                    p_copy(jp, k).wait_recv()

                @pl.when(has_right)
                def _():
                    p_tx[jp, k] = (local[jp, k] + p_rx[jp, k].astype(F32)).astype(BF16)
                    p_copy(jp, k).start()

        js = t - 1 - lag_s

        @pl.when(within(js))
        def _():
            for k in range(3):
                @pl.when(has_right)
                def _():
                    s_copy(js, k).wait_recv()

                @pl.when(has_left)
                def _():
                    s_tx[js, k] = (local[js, k] + s_rx[js, k].astype(F32)).astype(BF16)
                    s_copy(js, k).start()

        jf = t - 1 - lag

        @pl.when(within(jf))
        def _():
            q = core * steps + jf
            total = [
                local[jf, k] + p_rx[jf, k].astype(F32) + s_rx[jf, k].astype(F32) for k in range(3)
            ]
            for k, value in enumerate(nonlinear(*total)):
                act[q, k] = value
            act_copy(jf, core).start()
            store(q)
            backward(q)

        jb = jf - 1

        @pl.when(within(jb))
        def _():
            q = (1 - core) * steps + jb
            act_copy(jb, 1 - core).wait_recv()
            store(q)
            backward(q)

        return carry

    lax.fori_loop(0, steps + SKEW * last + 2, tick, 0)
    total = jnp.zeros((devices * tile_rows, half), F32)
    for kind, acc in enumerate((out_acc, dexp_acc)):
        for h in range(halves):
            total += jnp.dot(
                picks(kind, h, True),
                acc[:, h * half : (h + 1) * half].astype(BF16),
                preferred_element_type=F32,
            )
    results_ref[...] = total.astype(BF16).reshape(results_ref.shape)
    sent = pl.ds(0, devices - 1)
    pltpu.make_async_remote_copy(
        src_ref=pieces_ref.at[sent], dst_ref=pieces_rx.at[sent],
        send_sem=send_sem.at[4], recv_sem=piece_recv.at[0],
        device_id=(expert, mate), device_id_type=MESH,
    ).wait_send()
    remote(pair_tx, pair_rx, send_sem.at[0], pair_recv.at[0], mate).wait_send()

    @pl.when(has_right)
    def _():
        remote(p_tx, p_rx, send_sem.at[1], p_recv.at[0], right).wait_send()

    @pl.when(has_left)
    def _():
        remote(s_tx, s_rx, send_sem.at[2], s_recv.at[0], left).wait_send()

    mine = act.at[pl.ds(0, steps)]
    remote(mine, mine, send_sem.at[3], act_recv.at[0], mate).wait_send()
    pltpu.make_async_copy(act, act, store_sem).wait()


def plan(shards, rows, part, units):
    if shards % 2 or units % 256 or part % (16 // (2 * CAP) * 128):
        return None
    for width in (256, 128):
        if (units // 2) % width:
            continue
        held = 3 * part * units * 2 + 3 * rows * units * (2 + 2 + 6 * 1) + 2 * rows * part * (4 + 8)
        if held <= 55 * 2**20:
            return width
    return None


def expert_core(tokens, cotangent, slot_index, route_weight, w_gate, w_up, w_down, width):
    shards = lax.axis_size("shard")
    devices = lax.axis_size("expert") * shards
    rows = devices * CAP
    part, units = w_gate.shape
    halves = 16 // (2 * CAP)
    pieces = jax.ShapeDtypeStruct((devices, 16, part // halves), BF16)
    steps = units // 2 // width
    chips = shards // 2
    anywhere = pl.BlockSpec(memory_space=pl.ANY)
    vmem = pl.BlockSpec(memory_space=pltpu.VMEM)
    block = (steps, 3, rows, width)
    dma = pltpu.SemaphoreType.DMA
    return pl.pallas_call(
        functools.partial(core_kernel, chips, steps, width),
        out_shape=[jax.ShapeDtypeStruct((rows, units), BF16)] * 3
        + [jax.ShapeDtypeStruct((rows, part), BF16)] * 2
        + [pieces],
        in_specs=[vmem] * 4 + [anywhere] * 3,
        out_specs=[anywhere] * 3 + [vmem] * 3,
        scratch_shapes=[
            pltpu.VMEM(pieces.shape, BF16),
            pltpu.VMEM(pieces.shape, BF16),
            pltpu.VMEM((2 * steps, 3, part, width), BF16),
            pltpu.VMEM(block, BF16),
            pltpu.VMEM(block, BF16),
            pltpu.VMEM(block, F32),
            pltpu.VMEM(block, BF16),
            pltpu.VMEM(block, BF16),
            pltpu.VMEM(block, BF16),
            pltpu.VMEM(block, BF16),
            pltpu.VMEM((2 * steps, 3, rows, width), BF16),
            pltpu.VMEM((rows, part), F32),
            pltpu.VMEM((rows, part), F32),
            dma((2 * steps,)),
            dma((devices,)),
            dma((steps,)),
            dma((3 * steps,)),
            dma((3 * steps,)),
            dma((steps,)),
            dma((5,)),
            dma,
        ],
        compiler_params=pltpu.CompilerParams(
            collective_id=0, has_side_effects=True, vmem_limit_bytes=VMEM_BYTES
        ),
        name="expert_core",
    )(tokens, cotangent, slot_index, route_weight, w_gate, w_up, w_down)


def expert_plain(x_rows, d_rows, w_gate, w_up, w_down):
    rows = x_rows.shape[0]

    def partial(left, right):
        return jnp.dot(left, right, preferred_element_type=F32).astype(BF16)

    parts = jnp.concatenate(
        [partial(x_rows, w_gate), partial(x_rows, w_up), partial(d_rows, w_down)], axis=0
    )
    summed = lax.psum_scatter(parts, "shard", scatter_dimension=0, tiled=True)
    full = lax.all_gather(summed, "shard", axis=0, tiled=True).astype(F32)
    hidden, d_gate, d_up = nonlinear(full[:rows], full[rows : 2 * rows], full[2 * rows :])
    expert_out = back(hidden, w_down).astype(BF16)
    d_expert = (back(d_gate, w_gate) + back(d_up, w_up)).astype(BF16)
    return hidden, d_gate, d_up, expert_out, d_expert


def per_device(tokens, cotangent, expert_ids, slot_ids, route_weight, w_gate, w_up, w_down):
    experts = lax.axis_size("expert")
    shards = lax.axis_size("shard")
    slots_all = experts * CAP
    rows = experts * shards * CAP
    width = tokens.shape[1]
    part = width // shards
    slot_index = expert_ids * CAP + slot_ids
    columns = jnp.arange(slots_all, dtype=jnp.int32)
    slot_match = (slot_index[:, :, None] == columns[None, None, :]).astype(jnp.float32)
    dispatch = jnp.sum(slot_match, axis=1).astype(jnp.bfloat16)
    combine = jnp.sum(slot_match * route_weight[:, :, None], axis=1)
    hidden_units = w_gate.shape[2]
    devices = experts * shards
    width_step = plan(shards, rows, part, hidden_units)
    halves = 16 // (2 * CAP) if width_step else 1

    if width_step:
        hidden, d_gate, d_up, x_rows, d_rows, results = expert_core(
            tokens, cotangent, slot_index, route_weight,
            w_gate[0], w_up[0], w_down[0], width_step,
        )
    else:
        x_slots = jnp.einsum("tc,td->cd", dispatch, tokens, preferred_element_type=jnp.float32).astype(
            jnp.bfloat16
        )
        d_slots = jnp.dot(
            combine.T, cotangent.astype(jnp.float32), precision=lax.Precision.HIGHEST
        ).astype(jnp.bfloat16)
        both = jnp.stack([x_slots, d_slots]).reshape(
            2, experts, CAP, shards, halves, part // halves
        )
        pieces = both.transpose(1, 3, 4, 0, 2, 5).reshape(
            devices, halves * 2 * CAP, part // halves
        )
        arrived = lax.all_to_all(pieces, BOTH, split_axis=0, concat_axis=0, tiled=True)
        x_rows = arrived[:, :CAP].reshape(rows, part)
        d_rows = arrived[:, CAP:].reshape(rows, part)
        hidden, d_gate, d_up, expert_out, d_expert = expert_plain(
            x_rows, d_rows, w_gate[0], w_up[0], w_down[0]
        )
        results = jnp.concatenate(
            [expert_out.reshape(-1, CAP, part), d_expert.reshape(-1, CAP, part)], axis=1
        )
    returned = lax.all_to_all(results, BOTH, split_axis=0, concat_axis=0, tiled=True)
    returned = returned.reshape(experts, shards, halves, 2, CAP, part // halves)
    returned = returned.transpose(3, 0, 4, 1, 2, 5).reshape(2, slots_all, width)
    layer_out = jnp.dot(
        combine, returned[0].astype(jnp.float32), precision=lax.Precision.HIGHEST
    ).astype(jnp.bfloat16)
    d_tokens = jnp.dot(
        dispatch, returned[1], preferred_element_type=jnp.float32
    ).astype(jnp.bfloat16)

    def grad(left, right):
        return jnp.einsum("rd,rf->df", left, right, preferred_element_type=jnp.float32).astype(
            jnp.bfloat16
        )

    return (
        layer_out,
        d_tokens,
        grad(x_rows, d_gate)[None],
        grad(x_rows, d_up)[None],
        grad(d_rows, hidden)[None],
    )


def solution(mesh):
    tok = P(BOTH, None)
    wt = P("expert", "shard", None)
    return jax.shard_map(
        per_device,
        mesh=mesh,
        in_specs=(tok,) * 5 + (wt,) * 3,
        out_specs=(tok,) * 2 + (wt,) * 3,
        check_vma=False,
    )
```
